256 devices in a mesh: win: 32 (over z, y_lo, core), chan: 8 (over x, y_hi).
Axes of the slice: x: 4, y: 4 (y_hi: 2, y_lo: 2; y = y_hi * 2 + y_lo), z: 8, core: 2. Of those that a mesh axis runs over, the one named last changes fastest.
Arguments:
- traces: bfloat16 [256, 1024, 4096], P('win', 'chan'), may hold values from -6 to 6
- source_block: int32 [3], replicated, may hold values from 0 to 7, as said below
- pair_source: int32 [3, 4096], P(None, 'chan'), may hold values from 0 to 127
- pair_receiver: int32 [3, 4096], P(None, 'chan'), may hold values from 0 to 127
- pair_bin: int32 [3, 4096], P(None, 'chan'), may hold values from 0 to 1023, as said below
- bin_slot: int32 [1024], replicated, may hold values from 0 to 1023, as said below
Outputs:
- stacks: float32 [3, 4096, 1024], P(None, 'win', 'chan')
The draws below stay inside these ranges and needn't reach their ends.
Inputs may be any that keep to these rules, and one draw needn't show every extreme that they name: `source_block`: not every step names the same block; some step names block 0 and some step block 8 - 1. `pair_bin`: among the 512 pairs of one index of chan in a step, at most 128 have bins with bin_slot // 128 equal to one owner; in every step one owner gets exactly 128 from every index of chan. `bin_slot`: each bin has its own row.
All inputs are finite; a program needn't handle non-finite values.
Results may differ from the reference program's by a relative error of at most 0.0056.
Values may be sent and summed in bfloat16 or wider, within the bound.
No kernel may reach another device: no remote copies, remote signals or barrier semaphores. Data moves between devices by JAX's collectives and lax.ppermute only.
A program may use at most 64 MiB of HBM per device.

```python
import math
import jax
import jax.numpy as jnp
from jax import lax

WLEN = 4096
F = 128
FREQ0 = 256
LAGS = 4096
CH_DEV = 128
BIN_DEV = 128
STEPS = 3
WIN_DEV = 8
P_DEV = 512
CAP = 128
PAIRS = 4096
CHANNELS = 1024
WINDOWS = 256
BINS = 1024
N_WIN = 32
N_CHAN = 8


def draw_source_block(key, part):
    values = jax.random.randint(jax.random.fold_in(key, 301), (STEPS,), 0, N_CHAN).astype(jnp.int32)
    values = values.at[0].set(N_CHAN - 1).at[1].set(0)
    order = jax.random.permutation(jax.random.fold_in(key, 302), STEPS)
    return values[order].astype(jnp.int32)


def routing_tables(key):
    slot_of_bin = jax.random.permutation(jax.random.fold_in(key, 101), BINS).astype(jnp.int32)
    bin_of_slot = jnp.argsort(slot_of_bin, stable=True).astype(jnp.int32)
    blocks = PAIRS // P_DEV
    others = blocks - 1
    busy = jax.random.randint(jax.random.fold_in(key, 102), (STEPS,), 0, blocks).astype(jnp.int32)
    rows_all = []
    for section_index in range(STEPS):
        pieces = []
        for block_index in range(blocks):
            block_key = jax.random.fold_in(jax.random.fold_in(key, 200 + section_index), block_index)
            pool = jax.random.permutation(jax.random.fold_in(block_key, 1), others * CAP)[:P_DEV - CAP]
            other_owner = (pool // CAP).astype(jnp.int32)
            other_owner = other_owner + (other_owner >= busy[section_index]).astype(jnp.int32)
            owners = jnp.concatenate([jnp.full((CAP,), busy[section_index], jnp.int32), other_owner])
            owners = jax.random.permutation(jax.random.fold_in(block_key, 2), owners)
            row_in_owner = jax.random.randint(jax.random.fold_in(block_key, 3), (P_DEV,), 0, BIN_DEV).astype(jnp.int32)
            pieces.append(bin_of_slot[owners * BIN_DEV + row_in_owner])
        rows_all.append(jnp.concatenate(pieces))
    return (slot_of_bin, jnp.stack(rows_all).astype(jnp.int32))


def draw_pair_bin(key, part):
    return routing_tables(key)[1]


def draw_bin_slot(key, part):
    return routing_tables(key)[0]


def touch_ends(array, key, smallest, high):
    shape = array.shape
    place = [jax.random.randint(jax.random.fold_in(key, axis), (), 0, shape[axis]) for axis in range(len(shape))]
    array = array.at[tuple(place)].set(smallest)
    longest = shape.index(max(shape))
    place[longest] = (place[longest] + 1) % shape[longest]
    return array.at[tuple(place)].set(high)


def block_levels(own_key, shape, cuts, low, largest):
    level = 1.0
    for position, shards_of in cuts:
        heights = jax.random.uniform(jax.random.fold_in(jax.random.fold_in(own_key, 6), position), (shards_of,), jnp.float32, low / len(cuts), largest / len(cuts))
        level = level * jnp.repeat(jnp.exp(heights), shape[position] // shards_of).reshape((-1,) + (1,) * (len(shape) - 1 - position))
    return level


def scatter_about(stream_key, shape, deviation, reach, split=(), kind=jnp.bfloat16):
    entries = deviation * jax.random.normal(stream_key, shape, jnp.float32)
    if split:
        entries = entries * block_levels(stream_key, shape, split, -0.22, 0.18)
    return jnp.clip(entries, -reach, reach).astype(kind)


def setup_inputs(seed: int = 0) -> dict:
    splits = jax.random.split(jax.random.key(seed), 7)
    traces = scatter_about(splits[0], (WINDOWS, CHANNELS, WLEN), 1.0, 6.0, ((0, 32), (1, 8)))
    source_block = draw_source_block(jax.random.fold_in(splits[6], 71), 0)
    pair_source = touch_ends(jax.random.randint(splits[2], (STEPS, PAIRS), 0, CH_DEV), jax.random.fold_in(splits[2], 1), 0, CH_DEV - 1).astype(jnp.int32)
    pair_receiver = touch_ends(jax.random.randint(splits[3], (STEPS, PAIRS), 0, CH_DEV), jax.random.fold_in(splits[3], 1), 0, CH_DEV - 1).astype(jnp.int32)
    pair_bin = draw_pair_bin(jax.random.fold_in(splits[6], 71), 0)
    bin_slot = draw_bin_slot(jax.random.fold_in(splits[6], 71), 0)
    return dict(traces=traces, source_block=source_block, pair_source=pair_source, pair_receiver=pair_receiver, pair_bin=pair_bin, bin_slot=bin_slot)


def forward_table():
    samples = jnp.arange(WLEN, dtype=jnp.int32)
    freq_ids = FREQ0 + jnp.arange(F, dtype=jnp.int32)
    phases = samples[:, None] * freq_ids[None, :] % WLEN
    angles = phases.astype(jnp.float32) * (2.0 * math.pi / WLEN)
    return jnp.concatenate([jnp.cos(angles), -jnp.sin(angles)], axis=1).astype(jnp.bfloat16)

def lag_table(offset, length, norm_scale):
    samples = offset + jnp.arange(length, dtype=jnp.int32)
    freq_ids = FREQ0 + jnp.arange(F, dtype=jnp.int32)
    phases = freq_ids[:, None] * (samples[None, :] + (WLEN - LAGS // 2)) % WLEN
    angles = phases.astype(jnp.float32) * (2.0 * math.pi / WLEN)
    return jnp.concatenate([jnp.cos(angles), -jnp.sin(angles)], axis=0) * norm_scale

def cross_spectra(src_spec, rec_spec):
    src_re, src_im = (src_spec[..., :F], src_spec[..., F:])
    rec_re, rec_im = (rec_spec[..., :F], rec_spec[..., F:])
    real_part = lax.optimization_barrier(jnp.sum(src_re * rec_re + src_im * rec_im, axis=0))
    imag_part = lax.optimization_barrier(jnp.sum(src_re * rec_im - src_im * rec_re, axis=0))
    return jnp.concatenate([real_part, imag_part], axis=-1)

def reference(traces, source_block, pair_source, pair_receiver, pair_bin, bin_slot):
    forward_basis = forward_table()

    def whiten_window(window_rows):
        spectra = jnp.dot(window_rows, forward_basis, preferred_element_type=jnp.float32)
        power = lax.optimization_barrier(jnp.mean(spectra * spectra, axis=-1, keepdims=True))
        return (spectra * lax.rsqrt(power + 1e-06)).astype(jnp.bfloat16)
    whitened = lax.map(whiten_window, traces)
    groups = whitened.reshape(N_WIN, WIN_DEV, CHANNELS, 2 * F)
    lag_basis = lag_table(jnp.int32(0), LAGS, 1.0 / math.sqrt(2.0 * F * WINDOWS))
    results = []
    for section_index in range(STEPS):
        sources = source_block[section_index] * CH_DEV + pair_source[section_index]
        receivers = jnp.arange(PAIRS, dtype=jnp.int32) // P_DEV * CH_DEV + pair_receiver[section_index]
        slot_ids = bin_slot[pair_bin[section_index]]

        def group_sum(summed, window_group):
            src_spec = window_group[:, sources, :].astype(jnp.float32)
            rec_spec = window_group[:, receivers, :].astype(jnp.float32)
            rounded = cross_spectra(src_spec, rec_spec).astype(jnp.bfloat16)
            rounded = lax.optimization_barrier(rounded).astype(jnp.float32)
            return (summed + jax.ops.segment_sum(rounded, slot_ids, num_segments=BINS), None)
        binned = lax.scan(group_sum, jnp.zeros((BINS, 2 * F), jnp.float32), groups)[0]
        stacked = lax.dot_general(lag_basis, binned, (((0,), (1,)), ((), ())), precision=lax.Precision.HIGHEST)
        results.append(stacked)
    return jnp.stack(results)
```

```python
import math

import jax
import jax.numpy as jnp
import numpy as np
from jax import lax
from jax.experimental import pallas as pl
from jax.experimental.pallas import tpu as pltpu
from jax.sharding import PartitionSpec as P

WLEN = 4096
F = 128
FREQ0 = 256
LAGS = 4096
CH_DEV = 128
BIN_DEV = 128
STEPS = 3
WIN_DEV = 8
P_DEV = 512
BINS = 1024
N_WIN = 32
N_CHAN = 8

FG = F // N_CHAN
COLS = 2 * FG
ROWS = WIN_DEV * COLS
QUARTERS = P_DEV // 128
META = STEPS * 4 * QUARTERS
SUB = BIN_DEV // N_WIN
PART = STEPS * SUB
NT = (((1,), (1,)), ((), ()))
BF = jnp.bfloat16
F32 = jnp.float32


def column_order():
    group, part, freq = np.meshgrid(
        np.arange(N_CHAN), np.arange(2), np.arange(FG), indexing="ij"
    )
    return (part * F + group * FG + freq).reshape(-1)


def forward_rows():
    phases = (FREQ0 + np.arange(F))[:, None] * np.arange(WLEN)[None, :] % WLEN
    angles = phases.astype(np.float32) * np.float32(2.0 * math.pi / WLEN)
    rows = np.concatenate([np.cos(angles), -np.sin(angles)], axis=0)[column_order()]
    return rows.astype(BF)


def lag_rows(first_lag):
    lags = first_lag + jnp.arange(LAGS // N_WIN, dtype=jnp.int32)
    order = column_order()
    freq_ids = jnp.asarray(FREQ0 + order % F, jnp.int32)
    is_sin = jnp.asarray(order >= F)
    phases = freq_ids[None, :] * (lags[:, None] + (WLEN - LAGS // 2)) % WLEN
    angles = phases.astype(F32) * (2.0 * math.pi / WLEN)
    norm_scale = 1.0 / math.sqrt(2.0 * F * N_WIN * WIN_DEV)
    return jnp.where(is_sin[None, :], -jnp.sin(angles), jnp.cos(angles)) * norm_scale


def whiten_kernel(x_ref, table_ref, slot_ref, source_ref, receiver_ref, bin_ref, out_ref):
    step = pl.program_id(0)
    rows = x_ref[...].reshape(2 * CH_DEV, WLEN)
    spectra = lax.dot_general(table_ref[...], rows, NT, preferred_element_type=F32)
    power = jnp.sum(spectra * spectra, axis=0, keepdims=True) * (1.0 / (2 * F))
    whitened = (spectra * lax.rsqrt(power + 1e-06)).astype(BF)
    for half in range(2):
        first = pl.multiple_of((2 * step + half) * COLS, COLS)
        for group in range(N_CHAN):
            out_ref[group, pl.ds(first, COLS), :] = whitened[
                group * COLS : (group + 1) * COLS, half * CH_DEV : (half + 1) * CH_DEV
            ]

    @pl.when(step < STEPS)
    def _():
        bins = bin_ref[0]
        chosen = lax.broadcasted_iota(jnp.int32, (BINS, P_DEV), 0) == bins
        slots = jnp.sum(jnp.where(chosen, slot_ref[...], 0), axis=0, keepdims=True)
        owner = slots // BIN_DEV
        low = slots % BIN_DEV
        target = low // SUB * N_CHAN + owner
        lists = [source_ref[0], receiver_ref[0], target, low % SUB]
        block = jnp.concatenate(
            [v[:, q * 128 : (q + 1) * 128] for v in lists for q in range(QUARTERS)], axis=0
        )
        block = block.astype(F32).astype(BF)
        first = pl.multiple_of(ROWS + step * 16, 16)
        for group in range(N_CHAN):
            out_ref[group, pl.ds(first, 16), :] = block


def whiten(traces, pair_source, pair_receiver, pair_bin, bin_slot):
    lists = pl.BlockSpec((1, 1, P_DEV), lambda i: (jnp.minimum(i, STEPS - 1), 0, 0))
    return pl.pallas_call(
        whiten_kernel,
        grid=(WIN_DEV // 2,),
        in_specs=[
            pl.BlockSpec((2, CH_DEV, WLEN), lambda i: (i, 0, 0)),
            pl.BlockSpec((2 * F, WLEN), lambda i: (0, 0), pipeline_mode=pl.Buffered(1)),
            pl.BlockSpec((BINS, 1), lambda i: (0, 0), pipeline_mode=pl.Buffered(1)),
            lists,
            lists,
            lists,
        ],
        out_specs=pl.BlockSpec((N_CHAN, ROWS + META, CH_DEV), lambda i: (0, 0, 0)),
        out_shape=jax.ShapeDtypeStruct((N_CHAN, ROWS + META, CH_DEV), BF),
        compiler_params=pltpu.CompilerParams(vmem_limit_bytes=40 << 20),
    )(
        traces,
        jnp.asarray(forward_rows()),
        bin_slot.reshape(BINS, 1),
        pair_source.reshape(STEPS, 1, P_DEV),
        pair_receiver.reshape(STEPS, 1, P_DEV),
        pair_bin.reshape(STEPS, 1, P_DEV),
    )


def spread(row, count):
    index = lax.broadcasted_iota(jnp.int32, (count, row.shape[1]), 0).astype(F32)
    return jnp.where(index == row, 1.0, 0.0).astype(BF)


def pairs_kernel(block_ref, y_ref, out_ref, acc_ref):
    for s in range(STEPS):
        acc_ref[...] = jnp.zeros_like(acc_ref)
        source = y_ref[block_ref[s], :ROWS, :]

        def body(c, carry):
            lists = y_ref[c, pl.ds(ROWS + s * 16, 16), :].astype(F32)

            def row(kind):
                return jnp.concatenate(
                    [lists[kind * QUARTERS + q : kind * QUARTERS + q + 1] for q in range(QUARTERS)],
                    axis=1,
                )

            a = jnp.dot(source, spread(row(0), CH_DEV), preferred_element_type=F32)
            b = jnp.dot(
                y_ref[c, :ROWS, :], spread(row(1), CH_DEV), preferred_element_type=F32
            )
            real_part = jnp.zeros((FG, P_DEV), F32)
            imag_part = jnp.zeros((FG, P_DEV), F32)
            for w in range(WIN_DEV):
                a_re, a_im = a[w * COLS : w * COLS + FG], a[w * COLS + FG : (w + 1) * COLS]
                b_re, b_im = b[w * COLS : w * COLS + FG], b[w * COLS + FG : (w + 1) * COLS]
                real_part += a_re * b_re + a_im * b_im
                imag_part += a_re * b_im - a_im * b_re
            partial = jnp.concatenate([real_part, imag_part], axis=0)
            low = row(3)
            placed = jnp.concatenate(
                [jnp.where(low == float(k), partial, 0.0) for k in range(SUB)], axis=0
            ).astype(BF)
            acc_ref[...] += lax.dot_general(
                spread(row(2), N_WIN * N_CHAN), placed, NT, preferred_element_type=F32
            )
            return carry

        lax.fori_loop(0, N_CHAN, body, 0)
        out_ref[:, s * 128 : (s + 1) * 128] = acc_ref[...].astype(BF)


def bin_pairs(source_block, blocks):
    return pl.pallas_call(
        pairs_kernel,
        in_specs=[
            pl.BlockSpec(memory_space=pltpu.SMEM),
            pl.BlockSpec(memory_space=pltpu.VMEM),
        ],
        out_specs=pl.BlockSpec(memory_space=pltpu.VMEM),
        out_shape=jax.ShapeDtypeStruct((N_WIN * N_CHAN, STEPS * SUB * COLS), BF),
        scratch_shapes=[pltpu.VMEM((N_WIN * N_CHAN, SUB * COLS), F32)],
        compiler_params=pltpu.CompilerParams(vmem_limit_bytes=32 << 20),
    )(source_block, blocks)


def on_device(traces, source_block, pair_source, pair_receiver, pair_bin, bin_slot):
    blocks = whiten(traces, pair_source, pair_receiver, pair_bin, bin_slot)
    blocks = lax.all_to_all(blocks, "chan", 0, 0, tiled=True)
    binned = bin_pairs(source_block, blocks)
    binned = binned.reshape(N_WIN * N_CHAN, STEPS, SUB * COLS)
    binned = lax.all_to_all(binned, ("win", "chan"), 0, 0, tiled=True)
    total = jnp.sum(
        binned.reshape(N_WIN, N_CHAN, STEPS, SUB, COLS).astype(F32), axis=0
    )
    total = total.transpose(1, 2, 0, 3).reshape(PART, 2 * F).astype(BF)
    total = jnp.broadcast_to(total[None], (N_WIN, PART, 2 * F))
    total = lax.all_to_all(total, "win", 0, 0, tiled=True)
    total = total.reshape(N_WIN, STEPS, SUB, 2 * F).transpose(1, 0, 2, 3)
    total = total.reshape(STEPS, BIN_DEV, 2 * F).astype(F32)
    basis = lag_rows(lax.axis_index("win") * (LAGS // N_WIN))
    return jnp.einsum("tj,sbj->stb", basis, total, precision=lax.Precision.HIGHEST)


def solution(mesh):
    placed = (P("win", "chan", None), P(), P(None, "chan"), P(None, "chan"), P(None, "chan"), P())
    return jax.shard_map(
        on_device, mesh=mesh, in_specs=placed, out_specs=P(None, "win", "chan"), check_vma=False
    )
```

```python
import math

import jax
import jax.numpy as jnp
import numpy as np
from jax import lax
from jax.experimental import pallas as pl
from jax.experimental.pallas import tpu as pltpu
from jax.sharding import Mesh
from jax.sharding import PartitionSpec as P

WLEN = 4096
F = 128
FREQ0 = 256
LAGS = 4096
CH_DEV = 128
BIN_DEV = 128
STEPS = 3
WIN_DEV = 8
P_DEV = 512
BINS = 1024
N_WIN = 32
N_CHAN = 8
N_B = 8
N_A = N_WIN // N_B

GROUPS = N_A * N_CHAN
FG = F // GROUPS
COLS = 2 * FG
HALF = WIN_DEV * FG
ROWS = 2 * HALF
META = 16
QUARTERS = P_DEV // 128
SUB = BIN_DEV // N_B
TARGETS = N_B * N_CHAN
KCOLS = N_CHAN * COLS
PACKED = STEPS * SUB // 2
NT = (((1,), (1,)), ((), ()))
BF = jnp.bfloat16
F32 = jnp.float32
VMEM = pl.BlockSpec(memory_space=pltpu.VMEM)
SMEM = pl.BlockSpec(memory_space=pltpu.SMEM)
ANY = pl.BlockSpec(memory_space=pl.ANY)


def forward_rows():
    phases = (FREQ0 + np.arange(F))[:, None] * np.arange(WLEN)[None, :] % WLEN
    angles = phases.astype(np.float32) * np.float32(2.0 * math.pi / WLEN)
    return np.concatenate([np.cos(angles), -np.sin(angles)], axis=0).astype(BF)


def lag_tables():
    shape = (N_A, 2, N_CHAN, 2, FG)
    a, _, k, part, f = np.meshgrid(*[np.arange(n) for n in shape], indexing="ij")
    freq = (FREQ0 + FG * (a * N_CHAN + k) + f).reshape(-1)
    part = part.reshape(-1)
    block = LAGS // N_WIN
    inner = 2.0 * math.pi / WLEN * (freq[None, :] * np.arange(block)[:, None] % WLEN)
    starts = np.arange(N_WIN)[:, None] * block + (WLEN - LAGS // 2)
    outer = 2.0 * math.pi / WLEN * (freq[None, :] * starts % WLEN)
    norm_scale = 1.0 / math.sqrt(2.0 * F * N_WIN * WIN_DEV)
    first = np.where(part == 0, np.cos(outer), -np.sin(outer)) * norm_scale
    second = np.where(part == 0, -np.sin(outer), -np.cos(outer)) * norm_scale
    tables = np.cos(inner), np.sin(inner), first, second
    return [t.astype(np.float32) for t in tables]


def whiten_kernel(
    place_ref, x_hbm, table_hbm, slot_ref, source_ref, receiver_ref, bin_ref,
    out_ref, x_ref, table_ref, even_ref, x_sem, table_sem,
):
    table_copy = pltpu.make_async_copy(table_hbm, table_ref, table_sem)
    x_copies = [
        pltpu.make_async_copy(x_hbm.at[pl.ds(2 * i, 2)], x_ref.at[pl.ds(2 * i, 2)], x_sem.at[i])
        for i in range(WIN_DEV // 2)
    ]
    table_copy.start()
    for copy in x_copies:
        copy.start()

    slots = slot_ref[...]
    owner, low = slots // BIN_DEV, slots % BIN_DEV
    target = low // 8 % N_B * N_CHAN + owner
    sub = low // 64 * 8 + low % 8
    tables = jnp.concatenate([target, sub], axis=0).astype(F32).astype(BF)
    lane = lax.broadcasted_iota(jnp.int32, (128, P_DEV), 0)
    high = lax.broadcasted_iota(jnp.int32, (8, P_DEV), 0)
    place = place_ref[0]
    pieces = []
    for s in range(STEPS):
        bins = bin_ref[s : s + 1, :]
        onehot = jnp.where(lane == bins % 128, 1.0, 0.0).astype(BF)
        found = jnp.dot(tables, onehot, preferred_element_type=F32)
        here = high == bins // 128
        targets = jnp.sum(jnp.where(here, found[:8], 0.0), axis=0, keepdims=True)
        subs = jnp.sum(jnp.where(here, found[8:], 0.0), axis=0, keepdims=True)
        row = jnp.where(
            place < 2,
            jnp.where(place == 0, source_ref[s : s + 1, :], receiver_ref[s : s + 1, :]).astype(F32),
            jnp.where(place == 2, targets, subs),
        )
        pieces += [row[:, q * 128 : (q + 1) * 128] for q in range(QUARTERS)]
    pieces.append(jnp.zeros((META - len(pieces), 128), F32))
    block = jnp.concatenate(pieces, axis=0).astype(BF)
    for group in range(GROUPS):
        out_ref[group, ROWS:, :] = block

    table_copy.wait()
    upper = lax.broadcasted_iota(jnp.int32, (1, 8, 128), 1) < FG
    for i in range(WIN_DEV // 2):
        x_copies[i].wait()
        rows = x_ref[2 * i : 2 * i + 2].reshape(2 * CH_DEV, WLEN)
        spectra = lax.dot_general(table_ref[...], rows, NT, preferred_element_type=F32)
        power = jnp.sum(spectra * spectra, axis=0, keepdims=True) * (1.0 / (2 * F))
        whitened = (spectra * lax.rsqrt(power + 1e-06)).reshape(2 * F // 8, 8, 2 * CH_DEV)
        first, second = whitened[:, :, :CH_DEV], whitened[:, :, CH_DEV:]
        ours = [
            jnp.where(upper, first, jnp.roll(second, FG, axis=1)),
            jnp.where(upper, jnp.roll(first, FG, axis=1), second),
        ]
        for g in range(2):
            if i % 2 == 0:
                even_ref[g] = ours[g]
            else:
                both = jnp.concatenate([even_ref[g], ours[g]], axis=1).astype(BF)
                at = i // 2 * 16
                for pair in range(GROUPS // 2):
                    group = 2 * pair + g
                    out_ref[group, at : at + 16, :] = both[pair]
                    out_ref[group, HALF + at : HALF + at + 16, :] = both[GROUPS // 2 + pair]


def whiten(place, traces, pair_source, pair_receiver, pair_bin, bin_slot):
    return pl.pallas_call(
        whiten_kernel,
        in_specs=[SMEM, ANY, ANY, VMEM, VMEM, VMEM, VMEM],
        out_specs=VMEM,
        out_shape=jax.ShapeDtypeStruct((GROUPS, ROWS + META, CH_DEV), BF),
        scratch_shapes=[
            pltpu.VMEM((WIN_DEV, CH_DEV, WLEN), BF),
            pltpu.VMEM((2 * F, WLEN), BF),
            pltpu.VMEM((2, 2 * F // 8, 8, CH_DEV), F32),
            pltpu.SemaphoreType.DMA((WIN_DEV // 2,)),
            pltpu.SemaphoreType.DMA(()),
        ],
        compiler_params=pltpu.CompilerParams(vmem_limit_bytes=56 << 20),
    )(
        place, traces, jnp.asarray(forward_rows()), bin_slot.reshape(8, 128),
        pair_source, pair_receiver, pair_bin,
    )


def pairs_kernel(block_ref, y_ref, out_ref, source_ref):
    index = lax.broadcasted_iota(jnp.int32, (128, 128), 0).astype(F32).astype(BF)
    low_half = lax.broadcasted_iota(jnp.int32, (8, P_DEV), 0) < FG
    lower_row = (lax.broadcasted_iota(jnp.int32, (16, 128), 0) // 8).astype(F32)
    one, zero = jnp.ones((), BF), jnp.zeros((), BF)

    def spread(row, count):
        columns = []
        for q in range(QUARTERS):
            entry = jnp.broadcast_to(row[q : q + 1], (16, 128)).astype(BF)
            entry = jnp.concatenate([entry] * (count // 16), axis=0)
            columns.append(jnp.where(index[:count] == entry, one, zero))
        return jnp.concatenate(columns, axis=1)

    for s in range(STEPS):
        block = block_ref[s]
        for a in range(N_A):
            source_ref[a * ROWS : (a + 1) * ROWS, :] = y_ref[a, block, :ROWS, :]

        def body(c, total):
            lists = [
                y_ref[kind, c, ROWS:, :].astype(F32)[s * QUARTERS : (s + 1) * QUARTERS]
                for kind in range(4)
            ]
            receiver = jnp.concatenate([y_ref[a, c, :ROWS, :] for a in range(N_A)], axis=0)
            u = jnp.dot(source_ref[...], spread(lists[0], CH_DEV), preferred_element_type=F32)
            v = jnp.dot(receiver, spread(lists[1], CH_DEV), preferred_element_type=F32)
            real_part = jnp.zeros((8, P_DEV), F32)
            imag_part = jnp.zeros((8, P_DEV), F32)
            for a in range(N_A):
                for r in range(0, HALF, 8):
                    at = a * ROWS + r
                    u_re, u_im = u[at : at + 8], u[at + HALF : at + HALF + 8]
                    v_re, v_im = v[at : at + 8], v[at + HALF : at + HALF + 8]
                    real_part += u_re * v_re + u_im * v_im
                    imag_part += u_re * v_im - u_im * v_re
            real_part += jnp.roll(real_part, FG, axis=0)
            imag_part += jnp.roll(imag_part, FG, axis=0)
            partial = jnp.where(low_half, real_part, imag_part)
            partial = jnp.concatenate([partial, partial], axis=0).astype(BF)
            placed = []
            for q in range(QUARTERS):
                sub = (jnp.broadcast_to(lists[3][q : q + 1], (16, 128)) - lower_row).astype(BF)
                values = partial[:, q * 128 : (q + 1) * 128]
                placed.append(
                    jnp.concatenate(
                        [
                            jnp.where(sub == jnp.full((16, 128), float(k), BF), values, zero)
                            for k in range(0, SUB, 2)
                        ],
                        axis=0,
                    )
                )
            placed = jnp.concatenate(placed, axis=1)
            return total + lax.dot_general(
                spread(lists[2], TARGETS), placed, NT, preferred_element_type=F32
            )

        total = lax.fori_loop(
            0, N_CHAN, body, jnp.zeros((TARGETS, SUB * COLS), F32), unroll=2
        )
        out_ref[:, s * 128 : (s + 1) * 128] = total.astype(BF)


def bin_pairs(source_block, chunks):
    return pl.pallas_call(
        pairs_kernel,
        in_specs=[SMEM, VMEM],
        out_specs=VMEM,
        out_shape=jax.ShapeDtypeStruct((TARGETS, STEPS * SUB * COLS), BF),
        scratch_shapes=[pltpu.VMEM((N_A * ROWS, CH_DEV), BF)],
        compiler_params=pltpu.CompilerParams(vmem_limit_bytes=32 << 20),
    )(source_block, chunks)


def sum_kernel(part_ref, out_ref):
    parts = part_ref[...].astype(F32).reshape(N_B, N_CHAN, STEPS * 128)
    total = jnp.sum(parts, axis=0).astype(BF).astype(F32)
    lane = lax.broadcasted_iota(jnp.int32, (SUB, 128), 1)
    here = lane // COLS == lax.broadcasted_iota(jnp.int32, (SUB, 128), 0)
    wide = []
    for k in range(N_CHAN):
        rows = [
            jnp.where(here, total[k : k + 1, s * 128 : (s + 1) * 128], 0.0) for s in range(STEPS)
        ]
        wide.append(jnp.concatenate(rows, axis=0).astype(BF))
    wide = jnp.concatenate(wide, axis=1)
    row = lax.broadcasted_iota(jnp.int32, (N_CHAN * 128, KCOLS), 0)
    column = lax.broadcasted_iota(jnp.int32, (N_CHAN * 128, KCOLS), 1)
    fold = (row % COLS == column % COLS) & (row // 128 == column // COLS)
    fold = jnp.where(fold, 1.0, 0.0).astype(BF)
    packed = jnp.dot(wide, fold, preferred_element_type=F32)
    packed = jnp.concatenate([packed[:PACKED], packed[PACKED:]], axis=1).astype(BF)
    for w in range(N_WIN):
        out_ref[w] = packed


def sum_windows(parts):
    return pl.pallas_call(
        sum_kernel,
        in_specs=[VMEM],
        out_specs=VMEM,
        out_shape=jax.ShapeDtypeStruct((N_WIN, PACKED, 128), BF),
    )(parts)


def lag_kernel(place_ref, bins_ref, cos_ref, sin_ref, first_ref, second_ref, out_ref):
    place = place_ref[0]
    basis = (
        cos_ref[...] * first_ref[pl.ds(place, 1), :]
        + sin_ref[...] * second_ref[pl.ds(place, 1), :]
    )
    upper = basis.astype(BF)
    rest = (basis - upper.astype(F32)).astype(BF)
    lane_half = lax.broadcasted_iota(jnp.int32, (64, 128), 1) // KCOLS
    for s in range(STEPS):
        pieces = []
        for part in range(2):
            first = s * SUB + part * 8
            half, at = first // PACKED, first % PACKED
            columns = []
            for a in range(N_A):
                rows = [
                    bins_ref[b * N_A + a].astype(F32)[at : at + 8] for b in range(N_B)
                ]
                rows = jnp.concatenate(rows, axis=0)
                columns.append(jnp.where(lane_half == half, rows, 0.0).astype(BF))
            pieces.append(jnp.concatenate(columns, axis=1))
        binned = jnp.concatenate(pieces, axis=0)
        out_ref[s] = lax.dot_general(
            upper, binned, NT, preferred_element_type=F32
        ) + lax.dot_general(rest, binned, NT, preferred_element_type=F32)


def project_lags(place, bins):
    return pl.pallas_call(
        lag_kernel,
        in_specs=[SMEM] + [VMEM] * 5,
        out_specs=VMEM,
        out_shape=jax.ShapeDtypeStruct((STEPS, LAGS // N_WIN, BIN_DEV), F32),
        compiler_params=pltpu.CompilerParams(vmem_limit_bytes=32 << 20),
    )(place, bins, *[jnp.asarray(t) for t in lag_tables()])


def on_device(traces, source_block, pair_source, pair_receiver, pair_bin, bin_slot):
    place_a = lax.axis_index("a").reshape(1)
    place_win = lax.axis_index(("b", "a")).reshape(1)
    chunks = whiten(place_a, traces, pair_source, pair_receiver, pair_bin, bin_slot)
    chunks = lax.all_to_all(chunks, ("a", "chan"), 0, 0, tiled=True)
    parts = bin_pairs(source_block, chunks.reshape(N_A, N_CHAN, ROWS + META, CH_DEV))
    parts = lax.all_to_all(
        parts.reshape(TARGETS, STEPS, 128), ("b", "chan"), 0, 0, tiled=True
    )
    bins = sum_windows(parts.reshape(TARGETS, STEPS * 128))
    bins = lax.all_to_all(bins, ("b", "a"), 0, 0, tiled=True)
    return project_lags(place_win, bins)


def solution(mesh):
    split = Mesh(mesh.devices.reshape(N_B, N_A, N_CHAN), ("b", "a", "chan"))
    win = ("b", "a")
    placed = (P(win, "chan", None), P(), P(None, "chan"), P(None, "chan"), P(None, "chan"), P())
    return jax.shard_map(
        on_device, mesh=split, in_specs=placed, out_specs=P(None, win, "chan"), check_vma=False
    )
```

```python
import math

import jax
import jax.numpy as jnp
import numpy as np
from jax import lax
from jax.experimental import pallas as pl
from jax.experimental.pallas import tpu as pltpu
from jax.sharding import Mesh
from jax.sharding import PartitionSpec as P

WLEN = 4096
F = 128
FREQ0 = 256
LAGS = 4096
CH_DEV = 128
BIN_DEV = 128
STEPS = 3
WIN_DEV = 8
P_DEV = 512
BINS = 1024
N_WIN = 32
N_CHAN = 8
N_B = 8
N_A = N_WIN // N_B

GROUPS = N_A * N_CHAN
FG = F // GROUPS
COLS = 2 * FG
HALF = WIN_DEV * FG
ROWS = 2 * HALF
META = 16
QUARTERS = P_DEV // 128
SUB = BIN_DEV // N_B
TARGETS = N_B * N_CHAN
KCOLS = N_CHAN * COLS
PACKED = STEPS * SUB // 2
NT = (((1,), (1,)), ((), ()))
BF = jnp.bfloat16
F32 = jnp.float32
VMEM = pl.BlockSpec(memory_space=pltpu.VMEM)
SMEM = pl.BlockSpec(memory_space=pltpu.SMEM)
HBM = pl.BlockSpec(memory_space=pltpu.HBM)


def forward_tables():
    freq = (FREQ0 + np.arange(F))[:, None]
    inner = 2.0 * math.pi / WLEN * (freq * np.arange(128)[None, :] % WLEN)
    outer = 2.0 * math.pi / WLEN * (freq * np.arange(0, WLEN, 128)[None, :] % WLEN)
    pad = np.zeros((F, 128 - 2 * outer.shape[1]))
    tables = np.cos(inner), np.sin(inner), np.cos(outer), np.sin(outer), pad
    return np.concatenate(tables, axis=1).astype(np.float32)


def lag_tables():
    shape = (N_A, 2, N_CHAN, 2, FG)
    a, _, k, part, f = np.meshgrid(*[np.arange(n) for n in shape], indexing="ij")
    freq = (FREQ0 + FG * (a * N_CHAN + k) + f).reshape(-1)
    part = part.reshape(-1)
    block = LAGS // N_WIN
    inner = 2.0 * math.pi / WLEN * (freq[None, :] * np.arange(block)[:, None] % WLEN)
    starts = np.arange(N_WIN)[:, None] * block + (WLEN - LAGS // 2)
    outer = 2.0 * math.pi / WLEN * (freq[None, :] * starts % WLEN)
    norm_scale = 1.0 / math.sqrt(2.0 * F * N_WIN * WIN_DEV)
    first = np.where(part == 0, np.cos(outer), -np.sin(outer)) * norm_scale
    second = np.where(part == 0, -np.sin(outer), -np.cos(outer)) * norm_scale
    tables = np.cos(inner), np.sin(inner), first, second
    return [t.astype(np.float32) for t in tables]


def whiten_kernel(
    place_ref, x_hbm, basis_hbm, slot_hbm, source_hbm, receiver_hbm, bin_hbm,
    out_ref, x_ref, basis_ref, slot_ref, source_ref, receiver_ref, bin_ref,
    table_ref, even_ref, x_sem, small_sem,
):
    small = [
        pltpu.make_async_copy(slot_hbm, slot_ref, small_sem.at[0]),
        pltpu.make_async_copy(source_hbm, source_ref, small_sem.at[1]),
        pltpu.make_async_copy(receiver_hbm, receiver_ref, small_sem.at[2]),
        pltpu.make_async_copy(bin_hbm, bin_ref, small_sem.at[3]),
        pltpu.make_async_copy(basis_hbm, basis_ref, small_sem.at[4]),
    ]
    x_copies = [
        pltpu.make_async_copy(x_hbm.at[pl.ds(2 * i, 2)], x_ref.at[pl.ds(2 * i, 2)], x_sem.at[i])
        for i in range(WIN_DEV // 2)
    ]
    for copy in small + x_copies[:2]:
        copy.start()
    for copy in small:
        copy.wait()

    slots = slot_ref[...]
    owner, low = slots // BIN_DEV, slots % BIN_DEV
    target = low // 8 % N_B * N_CHAN + owner
    sub = low // 64 * 8 + low % 8
    tables = jnp.concatenate([target, sub], axis=0).astype(F32).astype(BF)
    lane = lax.broadcasted_iota(jnp.int32, (128, P_DEV), 0)
    high = lax.broadcasted_iota(jnp.int32, (8, P_DEV), 0)
    place = place_ref[0]
    pieces = []
    for s in range(STEPS):
        bins = bin_ref[s : s + 1, :]
        onehot = jnp.where(lane == bins % 128, 1.0, 0.0).astype(BF)
        found = jnp.dot(tables, onehot, preferred_element_type=F32)
        here = high == bins // 128
        targets = jnp.sum(jnp.where(here, found[:8], 0.0), axis=0, keepdims=True)
        subs = jnp.sum(jnp.where(here, found[8:], 0.0), axis=0, keepdims=True)
        row = jnp.where(
            place < 2,
            jnp.where(place == 0, source_ref[s : s + 1, :], receiver_ref[s : s + 1, :]).astype(F32),
            jnp.where(place == 2, targets, subs),
        )
        pieces += [row[:, q * 128 : (q + 1) * 128] for q in range(QUARTERS)]
    pieces.append(jnp.zeros((META - len(pieces), 128), F32))
    block = jnp.concatenate(pieces, axis=0).astype(BF)
    for group in range(GROUPS):
        out_ref[group, ROWS:, :] = block

    for copy in x_copies[2:]:
        copy.start()
    cos_in, sin_in = basis_ref[:, :128], basis_ref[:, 128:256]
    starts = WLEN // 128
    for q in range(starts):
        cos_out = jnp.broadcast_to(basis_ref[:, 256 + q : 257 + q], (F, 128))
        sin_out = jnp.broadcast_to(basis_ref[:, 256 + starts + q : 257 + starts + q], (F, 128))
        lanes = slice(q * 128, (q + 1) * 128)
        table_ref[:F, lanes] = (cos_out * cos_in - sin_out * sin_in).astype(BF)
        table_ref[F:, lanes] = (-(sin_out * cos_in) - cos_out * sin_in).astype(BF)
    upper = lax.broadcasted_iota(jnp.int32, (1, 8, 128), 1) < FG
    for i in range(WIN_DEV // 2):
        if i % 2 == 0:
            x_copies[i].wait()
            x_copies[i + 1].wait()
        rows = x_ref[2 * i : 2 * i + 2].reshape(2 * CH_DEV, WLEN)
        spectra = lax.dot_general(table_ref[...], rows, NT, preferred_element_type=F32)
        power = jnp.sum(spectra * spectra, axis=0, keepdims=True) * (1.0 / (2 * F))
        whitened = (spectra * lax.rsqrt(power + 1e-06)).reshape(2 * F // 8, 8, 2 * CH_DEV)
        first, second = whitened[:, :, :CH_DEV], whitened[:, :, CH_DEV:]
        ours = [
            jnp.where(upper, first, jnp.roll(second, FG, axis=1)),
            jnp.where(upper, jnp.roll(first, FG, axis=1), second),
        ]
        for g in range(2):
            if i % 2 == 0:
                even_ref[g] = ours[g]
            else:
                both = jnp.concatenate([even_ref[g], ours[g]], axis=1).astype(BF)
                at = i // 2 * 16
                for pair in range(GROUPS // 2):
                    group = 2 * pair + g
                    out_ref[group, at : at + 16, :] = both[pair]
                    out_ref[group, HALF + at : HALF + at + 16, :] = both[GROUPS // 2 + pair]


def whiten(place, traces, pair_source, pair_receiver, pair_bin, bin_slot):
    return pl.pallas_call(
        whiten_kernel,
        in_specs=[SMEM] + [HBM] * 6,
        out_specs=VMEM,
        out_shape=jax.ShapeDtypeStruct((GROUPS, ROWS + META, CH_DEV), BF),
        scratch_shapes=[
            pltpu.VMEM((WIN_DEV, CH_DEV, WLEN), BF),
            pltpu.VMEM((F, 384), F32),
            pltpu.VMEM((8, 128), jnp.int32),
            pltpu.VMEM((STEPS, P_DEV), jnp.int32),
            pltpu.VMEM((STEPS, P_DEV), jnp.int32),
            pltpu.VMEM((STEPS, P_DEV), jnp.int32),
            pltpu.VMEM((2 * F, WLEN), BF),
            pltpu.VMEM((2, 2 * F // 8, 8, CH_DEV), F32),
            pltpu.SemaphoreType.DMA((WIN_DEV // 2,)),
            pltpu.SemaphoreType.DMA((5,)),
        ],
        compiler_params=pltpu.CompilerParams(vmem_limit_bytes=24 << 20),
    )(
        place,
        *[
            pltpu.with_memory_space_constraint(array, pltpu.HBM)
            for array in (
                traces, jnp.asarray(forward_tables()), bin_slot.reshape(8, 128),
                pair_source, pair_receiver, pair_bin,
            )
        ],
    )


def pairs_kernel(block_ref, y_ref, out_ref, source_ref, placed_ref, target_ref):
    index = lax.broadcasted_iota(jnp.int32, (128, 128), 0).astype(F32).astype(BF)
    low_half = lax.broadcasted_iota(jnp.int32, (8, P_DEV), 0) < FG
    lower_row = (lax.broadcasted_iota(jnp.int32, (16, 128), 0) // 8).astype(F32)
    one, zero = jnp.ones((), BF), jnp.zeros((), BF)

    def spread(row, count):
        columns = []
        for q in range(QUARTERS):
            entry = jnp.broadcast_to(row[q : q + 1], (16, 128)).astype(BF)
            entry = jnp.concatenate([entry] * (count // 16), axis=0)
            columns.append(jnp.where(index[:count] == entry, one, zero))
        return jnp.concatenate(columns, axis=1)

    for s in range(STEPS):
        block = block_ref[s]
        for a in range(N_A):
            source_ref[a * ROWS : (a + 1) * ROWS, :] = y_ref[a, block, :ROWS, :]

        def body(c, carry):
            lists = [
                y_ref[kind, c, ROWS:, :].astype(F32)[s * QUARTERS : (s + 1) * QUARTERS]
                for kind in range(4)
            ]
            receiver = jnp.concatenate([y_ref[a, c, :ROWS, :] for a in range(N_A)], axis=0)
            u = jnp.dot(source_ref[...], spread(lists[0], CH_DEV), preferred_element_type=F32)
            v = jnp.dot(receiver, spread(lists[1], CH_DEV), preferred_element_type=F32)
            real_part = jnp.zeros((8, P_DEV), F32)
            imag_part = jnp.zeros((8, P_DEV), F32)
            for a in range(N_A):
                for r in range(0, HALF, 8):
                    at = a * ROWS + r
                    u_re, u_im = u[at : at + 8], u[at + HALF : at + HALF + 8]
                    v_re, v_im = v[at : at + 8], v[at + HALF : at + HALF + 8]
                    real_part += u_re * v_re + u_im * v_im
                    imag_part += u_re * v_im - u_im * v_re
            real_part += pltpu.roll(real_part, FG, axis=0)
            imag_part += pltpu.roll(imag_part, FG, axis=0)
            partial = jnp.where(low_half, real_part, imag_part)
            partial = jnp.concatenate([partial, partial], axis=0).astype(BF)
            for q in range(QUARTERS):
                sub = (jnp.broadcast_to(lists[3][q : q + 1], (16, 128)) - lower_row).astype(BF)
                values = partial[:, q * 128 : (q + 1) * 128]
                lanes = pl.ds(pl.multiple_of(c * P_DEV + q * 128, 128), 128)
                for k in range(0, SUB, 2):
                    placed_ref[k * 8 : k * 8 + 16, lanes] = jnp.where(
                        sub == jnp.full((16, 128), float(k), BF), values, zero
                    )
            target_ref[:, pl.ds(pl.multiple_of(c * P_DEV, 128), P_DEV)] = spread(
                lists[2], TARGETS
            )
            return carry

        lax.fori_loop(0, N_CHAN, body, 0, unroll=8)
        out_ref[:, s * 128 : (s + 1) * 128] = lax.dot_general(
            target_ref[...], placed_ref[...], NT, preferred_element_type=F32
        ).astype(BF)


def bin_pairs(source_block, chunks):
    return pl.pallas_call(
        pairs_kernel,
        in_specs=[SMEM, VMEM],
        out_specs=VMEM,
        out_shape=jax.ShapeDtypeStruct((TARGETS, STEPS * SUB * COLS), BF),
        scratch_shapes=[
            pltpu.VMEM((N_A * ROWS, CH_DEV), BF),
            pltpu.VMEM((SUB * COLS, N_CHAN * P_DEV), BF),
            pltpu.VMEM((TARGETS, N_CHAN * P_DEV), BF),
        ],
        compiler_params=pltpu.CompilerParams(vmem_limit_bytes=32 << 20),
    )(source_block, chunks)


def sum_kernel(part_ref, out_ref):
    parts = part_ref[...].astype(F32).reshape(N_B, N_CHAN, STEPS, 128)
    total = jnp.sum(parts, axis=0).astype(BF).astype(F32)
    lane = lax.broadcasted_iota(jnp.int32, (SUB, 128), 1)
    here = lane // COLS == lax.broadcasted_iota(jnp.int32, (SUB, 128), 0)
    wide = []
    for k in range(N_CHAN):
        rows = [
            jnp.where(here, total[k, s : s + 1], 0.0) for s in range(STEPS)
        ]
        wide.append(jnp.concatenate(rows, axis=0).astype(BF))
    wide = jnp.concatenate(wide, axis=1)
    row = lax.broadcasted_iota(jnp.int32, (N_CHAN * 128, KCOLS), 0)
    column = lax.broadcasted_iota(jnp.int32, (N_CHAN * 128, KCOLS), 1)
    fold = (row % COLS == column % COLS) & (row // 128 == column // COLS)
    fold = jnp.where(fold, 1.0, 0.0).astype(BF)
    packed = jnp.dot(wide, fold, preferred_element_type=F32)
    packed = jnp.concatenate([packed[:PACKED], packed[PACKED:]], axis=1).astype(BF)
    for w in range(N_WIN):
        out_ref[w] = packed


def sum_windows(parts):
    return pl.pallas_call(
        sum_kernel,
        in_specs=[VMEM],
        out_specs=VMEM,
        out_shape=jax.ShapeDtypeStruct((N_WIN, PACKED, 128), BF),
        compiler_params=pltpu.CompilerParams(vmem_limit_bytes=8 << 20),
    )(parts)


def lag_kernel(place_ref, bins_ref, cos_ref, sin_ref, first_ref, second_ref, out_ref):
    place = place_ref[0]
    basis = (
        cos_ref[...] * first_ref[pl.ds(place, 1), :]
        + sin_ref[...] * second_ref[pl.ds(place, 1), :]
    )
    upper = basis.astype(BF)
    rest = (basis - upper.astype(F32)).astype(BF)
    lane_half = lax.broadcasted_iota(jnp.int32, (64, 128), 1) // KCOLS
    for s in range(STEPS):
        pieces = []
        for part in range(2):
            first = s * SUB + part * 8
            half, at = first // PACKED, first % PACKED
            columns = []
            for a in range(N_A):
                rows = [
                    bins_ref[b * N_A + a].astype(F32)[at : at + 8] for b in range(N_B)
                ]
                rows = jnp.concatenate(rows, axis=0)
                columns.append(jnp.where(lane_half == half, rows, 0.0).astype(BF))
            pieces.append(jnp.concatenate(columns, axis=1))
        binned = jnp.concatenate(pieces, axis=0)
        out_ref[s] = lax.dot_general(
            upper, binned, NT, preferred_element_type=F32
        ) + lax.dot_general(rest, binned, NT, preferred_element_type=F32)


def project_lags(place, bins):
    return pl.pallas_call(
        lag_kernel,
        in_specs=[SMEM] + [VMEM] * 5,
        out_specs=VMEM,
        out_shape=jax.ShapeDtypeStruct((STEPS, LAGS // N_WIN, BIN_DEV), F32),
        compiler_params=pltpu.CompilerParams(vmem_limit_bytes=32 << 20),
    )(place, bins, *[jnp.asarray(t) for t in lag_tables()])


def on_device(traces, source_block, pair_source, pair_receiver, pair_bin, bin_slot):
    place_a = lax.axis_index("a").reshape(1)
    place_win = lax.axis_index(("b", "a")).reshape(1)
    chunks = whiten(place_a, traces, pair_source, pair_receiver, pair_bin, bin_slot)
    chunks = lax.all_to_all(chunks, ("a", "chan"), 0, 0, tiled=True)
    parts = bin_pairs(source_block, chunks.reshape(N_A, N_CHAN, ROWS + META, CH_DEV))
    parts = lax.all_to_all(
        parts.reshape(TARGETS, STEPS, 128), ("b", "chan"), 0, 0, tiled=True
    )
    bins = sum_windows(parts)
    bins = lax.all_to_all(bins, ("b", "a"), 0, 0, tiled=True)
    return project_lags(place_win, bins)


def solution(mesh):
    split = Mesh(mesh.devices.reshape(N_B, N_A, N_CHAN), ("b", "a", "chan"))
    win = ("b", "a")
    placed = (P(win, "chan", None), P(), P(None, "chan"), P(None, "chan"), P(None, "chan"), P())
    return jax.shard_map(
        on_device, mesh=split, in_specs=placed, out_specs=P(None, win, "chan"), check_vma=False
    )
```

```python
import math

import jax
import jax.numpy as jnp
import numpy as np
from jax import lax
from jax.experimental import pallas as pl
from jax.experimental.pallas import tpu as pltpu
from jax.sharding import Mesh
from jax.sharding import PartitionSpec as P

WLEN = 4096
F = 128
FREQ0 = 256
LAGS = 4096
CH_DEV = 128
BIN_DEV = 128
STEPS = 3
WIN_DEV = 8
P_DEV = 512
BINS = 1024
N_WIN = 32
N_CHAN = 8
N_B = 8
N_A = N_WIN // N_B

GROUPS = N_A * N_CHAN
FG = F // GROUPS
COLS = 2 * FG
HALF = WIN_DEV * FG
ROWS = 2 * HALF
META = 16
QUARTERS = P_DEV // 128
OWNED = N_CHAN * COLS
NT = (((1,), (1,)), ((), ()))
BF = jnp.bfloat16
F32 = jnp.float32
VMEM = pl.BlockSpec(memory_space=pltpu.VMEM)
SMEM = pl.BlockSpec(memory_space=pltpu.SMEM)
HBM = pl.BlockSpec(memory_space=pltpu.HBM)


def forward_tables():
    freq = (FREQ0 + np.arange(F))[:, None]
    inner = 2.0 * math.pi / WLEN * (freq * np.arange(128)[None, :] % WLEN)
    outer = 2.0 * math.pi / WLEN * (freq * np.arange(0, WLEN, 128)[None, :] % WLEN)
    pad = np.zeros((F, 128 - 2 * outer.shape[1]))
    tables = np.cos(inner), np.sin(inner), np.cos(outer), np.sin(outer), pad
    return np.concatenate(tables, axis=1).astype(np.float32)


def lag_tables():
    shape = (N_A, N_CHAN, 2, FG)
    a, k, part, f = np.meshgrid(*[np.arange(n) for n in shape], indexing="ij")
    freq = (FREQ0 + FG * (a * N_CHAN + k) + f).reshape(-1)
    part = part.reshape(-1)
    block = LAGS // N_WIN
    inner = 2.0 * math.pi / WLEN * (freq[None, :] * np.arange(block)[:, None] % WLEN)
    starts = np.arange(N_WIN)[:, None] * block + (WLEN - LAGS // 2)
    outer = 2.0 * math.pi / WLEN * (freq[None, :] * starts % WLEN)
    norm_scale = 1.0 / math.sqrt(2.0 * F * N_WIN * WIN_DEV)
    first = np.where(part == 0, np.cos(outer), -np.sin(outer)) * norm_scale
    second = np.where(part == 0, -np.sin(outer), -np.cos(outer)) * norm_scale
    tables = np.cos(inner), np.sin(inner), first, second
    return [t.astype(np.float32) for t in tables]


def whiten_kernel(
    place_ref, x_hbm, basis_hbm, slot_hbm, source_hbm, receiver_hbm, bin_hbm,
    out_ref, x_ref, basis_ref, slot_ref, source_ref, receiver_ref, bin_ref,
    table_ref, even_ref, x_sem, small_sem,
):
    small = [
        pltpu.make_async_copy(slot_hbm, slot_ref, small_sem.at[0]),
        pltpu.make_async_copy(source_hbm, source_ref, small_sem.at[1]),
        pltpu.make_async_copy(receiver_hbm, receiver_ref, small_sem.at[2]),
        pltpu.make_async_copy(bin_hbm, bin_ref, small_sem.at[3]),
        pltpu.make_async_copy(basis_hbm, basis_ref, small_sem.at[4]),
    ]
    x_copies = [
        pltpu.make_async_copy(x_hbm.at[pl.ds(2 * i, 2)], x_ref.at[pl.ds(2 * i, 2)], x_sem.at[i])
        for i in range(WIN_DEV // 2)
    ]
    for copy in small + x_copies[:2]:
        copy.start()
    for copy in small:
        copy.wait()

    slots = slot_ref[...]
    tables = jnp.concatenate([slots % BIN_DEV, slots // BIN_DEV], axis=0).astype(F32).astype(BF)
    lane = lax.broadcasted_iota(jnp.int32, (128, P_DEV), 0)
    high = lax.broadcasted_iota(jnp.int32, (8, P_DEV), 0)
    place = place_ref[0] % N_A
    pieces = []
    for s in range(STEPS):
        bins = bin_ref[s : s + 1, :]
        onehot = jnp.where(lane == bins % 128, 1.0, 0.0).astype(BF)
        found = jnp.dot(tables, onehot, preferred_element_type=F32)
        here = high == bins // 128
        row_in_owner = jnp.sum(jnp.where(here, found[:8], 0.0), axis=0, keepdims=True)
        owner = jnp.sum(jnp.where(here, found[8:], 0.0), axis=0, keepdims=True)
        row = jnp.where(
            place < 2,
            jnp.where(place == 0, source_ref[s : s + 1, :], receiver_ref[s : s + 1, :]).astype(F32),
            jnp.where(place == 2, row_in_owner, owner),
        )
        pieces += [row[:, q * 128 : (q + 1) * 128] for q in range(QUARTERS)]
    pieces.append(jnp.zeros((META - len(pieces), 128), F32))
    block = jnp.concatenate(pieces, axis=0).astype(BF)
    for group in range(GROUPS):
        out_ref[group, ROWS:, :] = block

    for copy in x_copies[2:]:
        copy.start()
    cos_in, sin_in = basis_ref[:, :128], basis_ref[:, 128:256]
    starts = WLEN // 128
    for q in range(starts):
        cos_out = jnp.broadcast_to(basis_ref[:, 256 + q : 257 + q], (F, 128))
        sin_out = jnp.broadcast_to(basis_ref[:, 256 + starts + q : 257 + starts + q], (F, 128))
        lanes = slice(q * 128, (q + 1) * 128)
        table_ref[:F, lanes] = (cos_out * cos_in - sin_out * sin_in).astype(BF)
        table_ref[F:, lanes] = (-(sin_out * cos_in) - cos_out * sin_in).astype(BF)
    upper = lax.broadcasted_iota(jnp.int32, (1, 8, 128), 1) < FG
    for i in range(WIN_DEV // 2):
        if i % 2 == 0:
            x_copies[i].wait()
            x_copies[i + 1].wait()
        rows = x_ref[2 * i : 2 * i + 2].reshape(2 * CH_DEV, WLEN)
        spectra = lax.dot_general(table_ref[...], rows, NT, preferred_element_type=F32)
        power = jnp.sum(spectra * spectra, axis=0, keepdims=True) * (1.0 / (2 * F))
        whitened = (spectra * lax.rsqrt(power + 1e-06)).reshape(2 * F // 8, 8, 2 * CH_DEV)
        first, second = whitened[:, :, :CH_DEV], whitened[:, :, CH_DEV:]
        ours = [
            jnp.where(upper, first, jnp.roll(second, FG, axis=1)),
            jnp.where(upper, jnp.roll(first, FG, axis=1), second),
        ]
        for g in range(2):
            if i % 2 == 0:
                even_ref[g] = ours[g]
            else:
                both = jnp.concatenate([even_ref[g], ours[g]], axis=1).astype(BF)
                at = i // 2 * 16
                for pair in range(GROUPS // 2):
                    group = 2 * pair + g
                    out_ref[group, at : at + 16, :] = both[pair]
                    out_ref[group, HALF + at : HALF + at + 16, :] = both[GROUPS // 2 + pair]


def whiten(place, traces, pair_source, pair_receiver, pair_bin, bin_slot):
    return pl.pallas_call(
        whiten_kernel,
        in_specs=[SMEM] + [HBM] * 6,
        out_specs=VMEM,
        out_shape=jax.ShapeDtypeStruct((GROUPS, ROWS + META, CH_DEV), BF),
        scratch_shapes=[
            pltpu.VMEM((WIN_DEV, CH_DEV, WLEN), BF),
            pltpu.VMEM((F, 384), F32),
            pltpu.VMEM((8, 128), jnp.int32),
            pltpu.VMEM((STEPS, P_DEV), jnp.int32),
            pltpu.VMEM((STEPS, P_DEV), jnp.int32),
            pltpu.VMEM((STEPS, P_DEV), jnp.int32),
            pltpu.VMEM((2 * F, WLEN), BF),
            pltpu.VMEM((2, 2 * F // 8, 8, CH_DEV), F32),
            pltpu.SemaphoreType.DMA((WIN_DEV // 2,)),
            pltpu.SemaphoreType.DMA((5,)),
        ],
        compiler_params=pltpu.CompilerParams(vmem_limit_bytes=24 << 20),
    )(
        place,
        *[
            pltpu.with_memory_space_constraint(array, pltpu.HBM)
            for array in (
                traces, jnp.asarray(forward_tables()), bin_slot.reshape(8, 128),
                pair_source, pair_receiver, pair_bin,
            )
        ],
    )


def pairs_kernel(block_ref, y_ref, out_ref, source_ref, placed_ref, row_ref):
    index = lax.broadcasted_iota(jnp.int32, (128, 128), 0).astype(F32).astype(BF)
    low_half = lax.broadcasted_iota(jnp.int32, (8, P_DEV), 0) < FG
    lower_row = (lax.broadcasted_iota(jnp.int32, (16, 128), 0) // 8).astype(F32)
    one, zero = jnp.ones((), BF), jnp.zeros((), BF)

    def spread(row):
        columns = []
        for q in range(QUARTERS):
            entry = jnp.broadcast_to(row[q : q + 1], (16, 128)).astype(BF)
            entry = jnp.concatenate([entry] * 8, axis=0)
            columns.append(jnp.where(index == entry, one, zero))
        return jnp.concatenate(columns, axis=1)

    for s in range(STEPS):
        block = block_ref[s]
        for a in range(N_A):
            source_ref[a * ROWS : (a + 1) * ROWS, :] = y_ref[a, block, :ROWS, :]

        def body(c, carry):
            lists = [
                y_ref[kind, c, ROWS:, :].astype(F32)[s * QUARTERS : (s + 1) * QUARTERS]
                for kind in range(4)
            ]
            receiver = jnp.concatenate([y_ref[a, c, :ROWS, :] for a in range(N_A)], axis=0)
            u = jnp.dot(source_ref[...], spread(lists[0]), preferred_element_type=F32)
            v = jnp.dot(receiver, spread(lists[1]), preferred_element_type=F32)
            real_part = jnp.zeros((8, P_DEV), F32)
            imag_part = jnp.zeros((8, P_DEV), F32)
            for a in range(N_A):
                for r in range(0, HALF, 8):
                    at = a * ROWS + r
                    u_re, u_im = u[at : at + 8], u[at + HALF : at + HALF + 8]
                    v_re, v_im = v[at : at + 8], v[at + HALF : at + HALF + 8]
                    real_part += u_re * v_re + u_im * v_im
                    imag_part += u_re * v_im - u_im * v_re
            real_part += pltpu.roll(real_part, FG, axis=0)
            imag_part += pltpu.roll(imag_part, FG, axis=0)
            partial = jnp.where(low_half, real_part, imag_part)
            partial = jnp.concatenate([partial, partial], axis=0).astype(BF)
            for q in range(QUARTERS):
                owner = (jnp.broadcast_to(lists[3][q : q + 1], (16, 128)) - lower_row).astype(BF)
                values = partial[:, q * 128 : (q + 1) * 128]
                lanes = pl.ds(pl.multiple_of(c * P_DEV + q * 128, 128), 128)
                for k in range(0, N_CHAN, 2):
                    placed_ref[k * 8 : k * 8 + 16, lanes] = jnp.where(
                        owner == jnp.full((16, 128), float(k), BF), values, zero
                    )
            row_ref[:, pl.ds(pl.multiple_of(c * P_DEV, 128), P_DEV)] = spread(lists[2])
            return carry

        lax.fori_loop(0, N_CHAN, body, 0, unroll=8)
        binned = lax.dot_general(
            placed_ref[...], row_ref[...], NT, preferred_element_type=F32
        ).astype(BF)
        for b in range(N_B):
            out_ref[b, :, s * BIN_DEV : (s + 1) * BIN_DEV] = binned


def bin_pairs(source_block, chunks):
    return pl.pallas_call(
        pairs_kernel,
        in_specs=[SMEM, VMEM],
        out_specs=VMEM,
        out_shape=jax.ShapeDtypeStruct((N_B, OWNED, STEPS * BIN_DEV), BF),
        scratch_shapes=[
            pltpu.VMEM((N_A * ROWS, CH_DEV), BF),
            pltpu.VMEM((OWNED, N_CHAN * P_DEV), BF),
            pltpu.VMEM((BIN_DEV, N_CHAN * P_DEV), BF),
        ],
        compiler_params=pltpu.CompilerParams(vmem_limit_bytes=32 << 20),
    )(source_block, chunks)


def sum_kernel(part_ref, out_ref):
    total = part_ref[0].astype(F32)
    for b in range(1, N_B):
        total += part_ref[b].astype(F32)
    total = total.astype(BF)
    for a in range(N_A):
        out_ref[a] = total


def sum_windows(parts):
    return pl.pallas_call(
        sum_kernel,
        in_specs=[VMEM],
        out_specs=VMEM,
        out_shape=jax.ShapeDtypeStruct((N_A, OWNED, STEPS * BIN_DEV), BF),
        compiler_params=pltpu.CompilerParams(vmem_limit_bytes=8 << 20),
    )(parts)


def lag_kernel(place_ref, bins_ref, cos_ref, sin_ref, first_ref, second_ref, out_ref):
    place = place_ref[0]
    basis = (
        cos_ref[...] * first_ref[pl.ds(place, 1), :]
        + sin_ref[...] * second_ref[pl.ds(place, 1), :]
    )
    upper = basis.astype(BF)
    rest = (basis - upper.astype(F32)).astype(BF)
    bins = bins_ref[...]
    stacks = jnp.dot(upper, bins, preferred_element_type=F32) + jnp.dot(
        rest, bins, preferred_element_type=F32
    )
    for s in range(STEPS):
        out_ref[s] = stacks[:, s * BIN_DEV : (s + 1) * BIN_DEV]


def project_lags(place, bins):
    return pl.pallas_call(
        lag_kernel,
        in_specs=[SMEM] + [VMEM] * 5,
        out_specs=VMEM,
        out_shape=jax.ShapeDtypeStruct((STEPS, LAGS // N_WIN, BIN_DEV), F32),
        compiler_params=pltpu.CompilerParams(vmem_limit_bytes=16 << 20),
    )(place, bins, *[jnp.asarray(t) for t in lag_tables()])


def on_device(traces, source_block, pair_source, pair_receiver, pair_bin, bin_slot):
    place = lax.axis_index(("b", "a")).reshape(1)
    chunks = whiten(place, traces, pair_source, pair_receiver, pair_bin, bin_slot)
    chunks = lax.all_to_all(chunks, ("a", "chan"), 0, 0, tiled=True)
    parts = bin_pairs(source_block, chunks.reshape(N_A, N_CHAN, ROWS + META, CH_DEV))
    parts = lax.all_to_all(parts, "b", 0, 0, tiled=True)
    bins = sum_windows(parts).reshape(GROUPS, COLS, STEPS * BIN_DEV)
    bins = lax.all_to_all(bins, ("a", "chan"), 0, 0, tiled=True)
    return project_lags(place, bins.reshape(2 * F, STEPS * BIN_DEV))


def solution(mesh):
    split = Mesh(mesh.devices.reshape(N_B, N_A, N_CHAN), ("b", "a", "chan"))
    win = ("b", "a")
    placed = (P(win, "chan", None), P(), P(None, "chan"), P(None, "chan"), P(None, "chan"), P())
    return jax.shard_map(
        on_device, mesh=split, in_specs=placed, out_specs=P(None, win, "chan"), check_vma=False
    )
```

```python
import math

import jax
import jax.numpy as jnp
import numpy as np
from jax import lax
from jax.experimental import pallas as pl
from jax.experimental.pallas import tpu as pltpu
from jax.sharding import Mesh
from jax.sharding import PartitionSpec as P

WLEN = 4096
F = 128
FREQ0 = 256
LAGS = 4096
CH_DEV = 128
BIN_DEV = 128
STEPS = 3
WIN_DEV = 8
P_DEV = 512
BINS = 1024
N_WIN = 32
N_CHAN = 8
N_B = 8
N_A = N_WIN // N_B

GROUPS = N_A * N_CHAN
FG = F // GROUPS
COLS = 2 * FG
HALF = WIN_DEV * FG
ROWS = 2 * HALF
META = 16
QUARTERS = P_DEV // 128
OWNED = N_CHAN * COLS
NT = (((1,), (1,)), ((), ()))
BF = jnp.bfloat16
F32 = jnp.float32
VMEM = pl.BlockSpec(memory_space=pltpu.VMEM)
SMEM = pl.BlockSpec(memory_space=pltpu.SMEM)
HBM = pl.BlockSpec(memory_space=pltpu.HBM)


def forward_tables():
    freq = (FREQ0 + np.arange(F))[:, None]
    inner = 2.0 * math.pi / WLEN * (freq * np.arange(128)[None, :] % WLEN)
    outer = 2.0 * math.pi / WLEN * (freq * np.arange(0, WLEN, 128)[None, :] % WLEN)
    pad = np.zeros((F, 128 - 2 * outer.shape[1]))
    tables = np.cos(inner), np.sin(inner), np.cos(outer), np.sin(outer), pad
    return np.concatenate(tables, axis=1).astype(np.float32)


def lag_tables():
    shape = (N_A, N_CHAN, 2, FG)
    a, k, part, f = np.meshgrid(*[np.arange(n) for n in shape], indexing="ij")
    freq = (FREQ0 + FG * (a * N_CHAN + k) + f).reshape(-1)
    part = part.reshape(-1)
    block = LAGS // N_WIN
    inner = 2.0 * math.pi / WLEN * (freq[None, :] * np.arange(block)[:, None] % WLEN)
    starts = np.arange(N_WIN)[:, None] * block + (WLEN - LAGS // 2)
    outer = 2.0 * math.pi / WLEN * (freq[None, :] * starts % WLEN)
    norm_scale = 1.0 / math.sqrt(2.0 * F * N_WIN * WIN_DEV)
    first = np.where(part == 0, np.cos(outer), -np.sin(outer)) * norm_scale
    second = np.where(part == 0, -np.sin(outer), -np.cos(outer)) * norm_scale
    tables = np.cos(inner), np.sin(inner), first, second
    return [t.astype(np.float32) for t in tables]


def whiten_kernel(
    place_ref, x_hbm, basis_hbm, slot_hbm, source_hbm, receiver_hbm, bin_hbm,
    out_ref, x_ref, basis_ref, slot_ref, source_ref, receiver_ref, bin_ref,
    table_ref, even_ref, x_sem, small_sem,
):
    small = [
        pltpu.make_async_copy(slot_hbm, slot_ref, small_sem.at[0]),
        pltpu.make_async_copy(source_hbm, source_ref, small_sem.at[1]),
        pltpu.make_async_copy(receiver_hbm, receiver_ref, small_sem.at[2]),
        pltpu.make_async_copy(bin_hbm, bin_ref, small_sem.at[3]),
        pltpu.make_async_copy(basis_hbm, basis_ref, small_sem.at[4]),
    ]
    x_copies = [
        pltpu.make_async_copy(x_hbm.at[pl.ds(2 * i, 2)], x_ref.at[pl.ds(2 * i, 2)], x_sem.at[i])
        for i in range(WIN_DEV // 2)
    ]
    for copy in small[-1:] + x_copies[:2] + small[:-1]:
        copy.start()
    small[-1].wait()
    cos_in, sin_in = basis_ref[:, :128], basis_ref[:, 128:256]
    starts = WLEN // 128
    for q in range(starts):
        if q == starts // 2:
            for copy in x_copies[2:]:
                copy.start()
        cos_out = jnp.broadcast_to(basis_ref[:, 256 + q : 257 + q], (F, 128))
        sin_out = jnp.broadcast_to(basis_ref[:, 256 + starts + q : 257 + starts + q], (F, 128))
        lanes = slice(q * 128, (q + 1) * 128)
        table_ref[:F, lanes] = (cos_out * cos_in - sin_out * sin_in).astype(BF)
        table_ref[F:, lanes] = (-(sin_out * cos_in) - cos_out * sin_in).astype(BF)
    def write_lists():
        slots = slot_ref[...]
        tables = jnp.concatenate([slots % BIN_DEV, slots // BIN_DEV], axis=0).astype(F32).astype(BF)
        lane = lax.broadcasted_iota(jnp.int32, (128, P_DEV), 0)
        high = lax.broadcasted_iota(jnp.int32, (8, P_DEV), 0)
        place = place_ref[0] % N_A
        pieces = []
        for s in range(STEPS):
            bins = bin_ref[s : s + 1, :]
            onehot = jnp.where(lane == bins % 128, 1.0, 0.0).astype(BF)
            found = jnp.dot(tables, onehot, preferred_element_type=F32)
            here = high == bins // 128
            row_in_owner = jnp.sum(jnp.where(here, found[:8], 0.0), axis=0, keepdims=True)
            owner = jnp.sum(jnp.where(here, found[8:], 0.0), axis=0, keepdims=True)
            row = jnp.where(
                place < 2,
                jnp.where(place == 0, source_ref[s : s + 1, :], receiver_ref[s : s + 1, :]).astype(F32),
                jnp.where(place == 2, row_in_owner, owner),
            )
            pieces += [row[:, q * 128 : (q + 1) * 128] for q in range(QUARTERS)]
        pieces.append(jnp.zeros((META - len(pieces), 128), F32))
        block = jnp.concatenate(pieces, axis=0).astype(BF)
        for group in range(GROUPS):
            out_ref[group, ROWS:, :] = block

    upper = lax.broadcasted_iota(jnp.int32, (1, 8, 128), 1) < FG
    for i in range(WIN_DEV // 2):
        if i % 2 == 0:
            x_copies[i].wait()
            x_copies[i + 1].wait()
        if i == 0:
            for copy in small[:-1]:
                copy.wait()
            write_lists()
        rows = x_ref[2 * i : 2 * i + 2].reshape(2 * CH_DEV, WLEN)
        spectra = lax.dot_general(table_ref[...], rows, NT, preferred_element_type=F32)
        power = jnp.sum(spectra * spectra, axis=0, keepdims=True) * (1.0 / (2 * F))
        whitened = (spectra * lax.rsqrt(power + 1e-06)).reshape(2 * F // 8, 8, 2 * CH_DEV)
        first, second = whitened[:, :, :CH_DEV], whitened[:, :, CH_DEV:]
        ours = [
            jnp.where(upper, first, jnp.roll(second, FG, axis=1)),
            jnp.where(upper, jnp.roll(first, FG, axis=1), second),
        ]
        for g in range(2):
            if i % 2 == 0:
                even_ref[g] = ours[g]
            else:
                both = jnp.concatenate([even_ref[g], ours[g]], axis=1).astype(BF)
                at = i // 2 * 16
                for pair in range(GROUPS // 2):
                    group = 2 * pair + g
                    out_ref[group, at : at + 16, :] = both[pair]
                    out_ref[group, HALF + at : HALF + at + 16, :] = both[GROUPS // 2 + pair]


def whiten(place, traces, pair_source, pair_receiver, pair_bin, bin_slot):
    return pl.pallas_call(
        whiten_kernel,
        in_specs=[SMEM] + [HBM] * 6,
        out_specs=VMEM,
        out_shape=jax.ShapeDtypeStruct((GROUPS, ROWS + META, CH_DEV), BF),
        scratch_shapes=[
            pltpu.VMEM((WIN_DEV, CH_DEV, WLEN), BF),
            pltpu.VMEM((F, 384), F32),
            pltpu.VMEM((8, 128), jnp.int32),
            pltpu.VMEM((STEPS, P_DEV), jnp.int32),
            pltpu.VMEM((STEPS, P_DEV), jnp.int32),
            pltpu.VMEM((STEPS, P_DEV), jnp.int32),
            pltpu.VMEM((2 * F, WLEN), BF),
            pltpu.VMEM((2, 2 * F // 8, 8, CH_DEV), F32),
            pltpu.SemaphoreType.DMA((WIN_DEV // 2,)),
            pltpu.SemaphoreType.DMA((5,)),
        ],
        compiler_params=pltpu.CompilerParams(vmem_limit_bytes=24 << 20),
    )(
        place,
        *[
            pltpu.with_memory_space_constraint(array, pltpu.HBM)
            for array in (
                traces, jnp.asarray(forward_tables()), bin_slot.reshape(8, 128),
                pair_source, pair_receiver, pair_bin,
            )
        ],
    )


def pairs_kernel(block_ref, y_ref, out_ref, source_ref, placed_ref, row_ref):
    index = lax.broadcasted_iota(jnp.int32, (128, 128), 0).astype(F32).astype(BF)
    low_half = lax.broadcasted_iota(jnp.int32, (8, P_DEV), 0) < FG
    lower_row = (lax.broadcasted_iota(jnp.int32, (16, 128), 0) // 8).astype(F32)
    one, zero = jnp.ones((), BF), jnp.zeros((), BF)

    def spread(row):
        columns = []
        for q in range(QUARTERS):
            entry = jnp.broadcast_to(row[q : q + 1], (16, 128)).astype(BF)
            entry = jnp.concatenate([entry] * 8, axis=0)
            columns.append(jnp.where(index == entry, one, zero))
        return jnp.concatenate(columns, axis=1)

    for s in range(STEPS):
        block = block_ref[s]
        for a in range(N_A):
            source_ref[a * ROWS : (a + 1) * ROWS, :] = y_ref[a, block, :ROWS, :]

        def body(c, carry):
            lists = [
                y_ref[kind, c, ROWS:, :].astype(F32)[s * QUARTERS : (s + 1) * QUARTERS]
                for kind in range(4)
            ]
            receiver = jnp.concatenate([y_ref[a, c, :ROWS, :] for a in range(N_A)], axis=0)
            u = jnp.dot(source_ref[...], spread(lists[0]), preferred_element_type=F32)
            v = jnp.dot(receiver, spread(lists[1]), preferred_element_type=F32)
            real_part = jnp.zeros((8, P_DEV), F32)
            imag_part = jnp.zeros((8, P_DEV), F32)
            for a in range(N_A):
                for r in range(0, HALF, 8):
                    at = a * ROWS + r
                    u_re, u_im = u[at : at + 8], u[at + HALF : at + HALF + 8]
                    v_re, v_im = v[at : at + 8], v[at + HALF : at + HALF + 8]
                    real_part += u_re * v_re + u_im * v_im
                    imag_part += u_re * v_im - u_im * v_re
            real_part += pltpu.roll(real_part, FG, axis=0)
            imag_part += pltpu.roll(imag_part, FG, axis=0)
            partial = jnp.where(low_half, real_part, imag_part)
            partial = jnp.concatenate([partial, partial], axis=0).astype(BF)
            for q in range(QUARTERS):
                owner = (jnp.broadcast_to(lists[3][q : q + 1], (16, 128)) - lower_row).astype(BF)
                values = partial[:, q * 128 : (q + 1) * 128]
                lanes = pl.ds(pl.multiple_of(c * P_DEV + q * 128, 128), 128)
                for k in range(0, N_CHAN, 2):
                    placed_ref[k * 8 : k * 8 + 16, lanes] = jnp.where(
                        owner == jnp.full((16, 128), float(k), BF), values, zero
                    )
            row_ref[:, pl.ds(pl.multiple_of(c * P_DEV, 128), P_DEV)] = spread(lists[2])
            return carry

        lax.fori_loop(0, N_CHAN, body, 0, unroll=8)
        binned = lax.dot_general(
            placed_ref[...], row_ref[...], NT, preferred_element_type=F32
        ).astype(BF)
        for b in range(N_B):
            out_ref[b, :, s * BIN_DEV : (s + 1) * BIN_DEV] = binned


def bin_pairs(source_block, chunks):
    return pl.pallas_call(
        pairs_kernel,
        in_specs=[SMEM, VMEM],
        out_specs=VMEM,
        out_shape=jax.ShapeDtypeStruct((N_B, OWNED, STEPS * BIN_DEV), BF),
        scratch_shapes=[
            pltpu.VMEM((N_A * ROWS, CH_DEV), BF),
            pltpu.VMEM((OWNED, N_CHAN * P_DEV), BF),
            pltpu.VMEM((BIN_DEV, N_CHAN * P_DEV), BF),
        ],
        compiler_params=pltpu.CompilerParams(vmem_limit_bytes=32 << 20),
    )(source_block, chunks)


def sum_kernel(part_ref, out_ref):
    total = part_ref[0].astype(F32)
    for b in range(1, N_B):
        total += part_ref[b].astype(F32)
    total = total.astype(BF)
    for a in range(N_A):
        out_ref[a] = total


def sum_windows(parts):
    return pl.pallas_call(
        sum_kernel,
        in_specs=[VMEM],
        out_specs=VMEM,
        out_shape=jax.ShapeDtypeStruct((N_A, OWNED, STEPS * BIN_DEV), BF),
        compiler_params=pltpu.CompilerParams(vmem_limit_bytes=8 << 20),
    )(parts)


def lag_kernel(place_ref, bins_ref, cos_ref, sin_ref, first_ref, second_ref, out_ref):
    place = place_ref[0]
    basis = (
        cos_ref[...] * first_ref[pl.ds(place, 1), :]
        + sin_ref[...] * second_ref[pl.ds(place, 1), :]
    )
    upper = basis.astype(BF)
    rest = (basis - upper.astype(F32)).astype(BF)
    bins = bins_ref[...]
    stacks = jnp.dot(upper, bins, preferred_element_type=F32) + jnp.dot(
        rest, bins, preferred_element_type=F32
    )
    for s in range(STEPS):
        out_ref[s] = stacks[:, s * BIN_DEV : (s + 1) * BIN_DEV]


def project_lags(place, bins):
    return pl.pallas_call(
        lag_kernel,
        in_specs=[SMEM] + [VMEM] * 5,
        out_specs=VMEM,
        out_shape=jax.ShapeDtypeStruct((STEPS, LAGS // N_WIN, BIN_DEV), F32),
        compiler_params=pltpu.CompilerParams(vmem_limit_bytes=16 << 20),
    )(place, bins, *[jnp.asarray(t) for t in lag_tables()])


def on_device(traces, source_block, pair_source, pair_receiver, pair_bin, bin_slot):
    place = lax.axis_index(("b", "a")).reshape(1)
    chunks = whiten(place, traces, pair_source, pair_receiver, pair_bin, bin_slot)
    chunks = lax.all_to_all(chunks, ("a", "chan"), 0, 0, tiled=True)
    parts = bin_pairs(source_block, chunks.reshape(N_A, N_CHAN, ROWS + META, CH_DEV))
    parts = lax.all_to_all(parts, "b", 0, 0, tiled=True)
    bins = sum_windows(parts).reshape(GROUPS, COLS, STEPS * BIN_DEV)
    bins = lax.all_to_all(bins, ("a", "chan"), 0, 0, tiled=True)
    return project_lags(place, bins.reshape(2 * F, STEPS * BIN_DEV))


def solution(mesh):
    split = Mesh(mesh.devices.reshape(N_B, N_A, N_CHAN), ("b", "a", "chan"))
    win = ("b", "a")
    placed = (P(win, "chan", None), P(), P(None, "chan"), P(None, "chan"), P(None, "chan"), P())
    return jax.shard_map(
        on_device, mesh=split, in_specs=placed, out_specs=P(None, win, "chan"), check_vma=False
    )
```

```python
import math

import jax
import jax.numpy as jnp
import numpy as np
from jax import lax
from jax.experimental import pallas as pl
from jax.experimental.pallas import tpu as pltpu
from jax.sharding import Mesh
from jax.sharding import PartitionSpec as P

WLEN = 4096
F = 128
FREQ0 = 256
LAGS = 4096
CH_DEV = 128
BIN_DEV = 128
STEPS = 3
WIN_DEV = 8
P_DEV = 512
BINS = 1024
N_WIN = 32
N_CHAN = 8
N_B = 8
N_A = N_WIN // N_B

GROUPS = N_A * N_CHAN
FG = F // GROUPS
COLS = 2 * FG
HALF = WIN_DEV * FG
ROWS = 2 * HALF
GROUPQ = 2
META = 16
QUARTERS = P_DEV // 128
OWNED = N_CHAN * COLS
NT = (((1,), (1,)), ((), ()))
BF = jnp.bfloat16
F32 = jnp.float32
VMEM = pl.BlockSpec(memory_space=pltpu.VMEM)
SMEM = pl.BlockSpec(memory_space=pltpu.SMEM)
HBM = pl.BlockSpec(memory_space=pltpu.HBM)


def forward_tables():
    freq = (FREQ0 + np.arange(F))[:, None]
    inner = 2.0 * math.pi / WLEN * (freq * np.arange(128)[None, :] % WLEN)
    outer = 2.0 * math.pi / WLEN * (freq * np.arange(0, WLEN, 128)[None, :] % WLEN)
    pad = np.zeros((F, 128 - 2 * outer.shape[1]))
    tables = np.cos(inner), np.sin(inner), np.cos(outer), np.sin(outer), pad
    return np.concatenate(tables, axis=1).astype(np.float32)


def lag_tables():
    shape = (N_A, N_CHAN, 2, FG)
    a, k, part, f = np.meshgrid(*[np.arange(n) for n in shape], indexing="ij")
    freq = (FREQ0 + FG * (a * N_CHAN + k) + f).reshape(-1)
    part = part.reshape(-1)
    block = LAGS // N_WIN
    inner = 2.0 * math.pi / WLEN * (freq[None, :] * np.arange(block)[:, None] % WLEN)
    starts = np.arange(N_WIN)[:, None] * block + (WLEN - LAGS // 2)
    outer = 2.0 * math.pi / WLEN * (freq[None, :] * starts % WLEN)
    norm_scale = 1.0 / math.sqrt(2.0 * F * N_WIN * WIN_DEV)
    first = np.where(part == 0, np.cos(outer), -np.sin(outer)) * norm_scale
    second = np.where(part == 0, -np.sin(outer), -np.cos(outer)) * norm_scale
    tables = np.cos(inner), np.sin(inner), first, second
    return [t.astype(np.float32) for t in tables]


def whiten_kernel(
    place_ref, x_hbm, basis_hbm, slot_hbm, source_hbm, receiver_hbm, bin_hbm,
    out_ref, x_ref, basis_ref, slot_ref, source_ref, receiver_ref, bin_ref,
    table_ref, even_ref, x_sem, small_sem,
):
    small = [
        pltpu.make_async_copy(slot_hbm, slot_ref, small_sem.at[0]),
        pltpu.make_async_copy(source_hbm, source_ref, small_sem.at[1]),
        pltpu.make_async_copy(receiver_hbm, receiver_ref, small_sem.at[2]),
        pltpu.make_async_copy(bin_hbm, bin_ref, small_sem.at[3]),
        pltpu.make_async_copy(basis_hbm, basis_ref, small_sem.at[4]),
    ]
    x_copies = [
        pltpu.make_async_copy(x_hbm.at[pl.ds(2 * i, 2)], x_ref.at[pl.ds(2 * i, 2)], x_sem.at[i])
        for i in range(WIN_DEV // 2)
    ]
    for copy in small[-1:] + x_copies[:2] + small[:-1]:
        copy.start()
    small[-1].wait()
    cos_in, sin_in = basis_ref[:, :128], basis_ref[:, 128:256]
    starts = WLEN // 128
    for q in range(starts):
        if q == starts // 2:
            for copy in x_copies[2:]:
                copy.start()
        cos_out = jnp.broadcast_to(basis_ref[:, 256 + q : 257 + q], (F, 128))
        sin_out = jnp.broadcast_to(basis_ref[:, 256 + starts + q : 257 + starts + q], (F, 128))
        lanes = slice(q * 128, (q + 1) * 128)
        table_ref[:F, lanes] = (cos_out * cos_in - sin_out * sin_in).astype(BF)
        table_ref[F:, lanes] = (-(sin_out * cos_in) - cos_out * sin_in).astype(BF)
    def write_lists():
        slots = slot_ref[...]
        tables = jnp.concatenate([slots % BIN_DEV, slots // BIN_DEV], axis=0).astype(F32).astype(BF)
        lane = lax.broadcasted_iota(jnp.int32, (128, P_DEV), 0)
        high = lax.broadcasted_iota(jnp.int32, (8, P_DEV), 0)
        place = place_ref[0] % N_A
        pieces = []
        for s in range(STEPS):
            bins = bin_ref[s : s + 1, :]
            onehot = jnp.where(lane == bins % 128, 1.0, 0.0).astype(BF)
            found = jnp.dot(tables, onehot, preferred_element_type=F32)
            here = high == bins // 128
            row_in_owner = jnp.sum(jnp.where(here, found[:8], 0.0), axis=0, keepdims=True)
            owner = jnp.sum(jnp.where(here, found[8:], 0.0), axis=0, keepdims=True)
            row = jnp.where(
                place < 2,
                jnp.where(place == 0, source_ref[s : s + 1, :], receiver_ref[s : s + 1, :]).astype(F32),
                jnp.where(place == 2, row_in_owner, owner),
            )
            pieces += [row[:, q * 128 : (q + 1) * 128] for q in range(QUARTERS)]
        pieces.append(jnp.zeros((META - len(pieces), 128), F32))
        block = jnp.concatenate(pieces, axis=0).astype(BF)
        for group in range(GROUPS):
            out_ref[group, ROWS:, :] = block

    upper = lax.broadcasted_iota(jnp.int32, (1, 8, 128), 1) < FG
    for i in range(WIN_DEV // 2):
        if i % 2 == 0:
            x_copies[i].wait()
            x_copies[i + 1].wait()
        if i == 0:
            for copy in small[:-1]:
                copy.wait()
            write_lists()
        rows = x_ref[2 * i : 2 * i + 2].reshape(2 * CH_DEV, WLEN)
        spectra = lax.dot_general(table_ref[...], rows, NT, preferred_element_type=F32)
        power = jnp.sum(spectra * spectra, axis=0, keepdims=True) * (1.0 / (2 * F))
        whitened = (spectra * lax.rsqrt(power + 1e-06)).reshape(2 * F // 8, 8, 2 * CH_DEV)
        first, second = whitened[:, :, :CH_DEV], whitened[:, :, CH_DEV:]
        ours = [
            jnp.where(upper, first, jnp.roll(second, FG, axis=1)),
            jnp.where(upper, jnp.roll(first, FG, axis=1), second),
        ]
        for g in range(2):
            if i % 2 == 0:
                even_ref[g] = ours[g]
            else:
                both = jnp.concatenate([even_ref[g], ours[g]], axis=1).astype(BF)
                at = i // 2 * 16
                for pair in range(GROUPS // 2):
                    group = 2 * pair + g
                    out_ref[group, at : at + 16, :] = both[pair]
                    out_ref[group, HALF + at : HALF + at + 16, :] = both[GROUPS // 2 + pair]


def whiten(place, traces, pair_source, pair_receiver, pair_bin, bin_slot):
    return pl.pallas_call(
        whiten_kernel,
        in_specs=[SMEM] + [HBM] * 6,
        out_specs=VMEM,
        out_shape=jax.ShapeDtypeStruct((GROUPS, ROWS + META, CH_DEV), BF),
        scratch_shapes=[
            pltpu.VMEM((WIN_DEV, CH_DEV, WLEN), BF),
            pltpu.VMEM((F, 384), F32),
            pltpu.VMEM((8, 128), jnp.int32),
            pltpu.VMEM((STEPS, P_DEV), jnp.int32),
            pltpu.VMEM((STEPS, P_DEV), jnp.int32),
            pltpu.VMEM((STEPS, P_DEV), jnp.int32),
            pltpu.VMEM((2 * F, WLEN), BF),
            pltpu.VMEM((2, 2 * F // 8, 8, CH_DEV), F32),
            pltpu.SemaphoreType.DMA((WIN_DEV // 2,)),
            pltpu.SemaphoreType.DMA((5,)),
        ],
        compiler_params=pltpu.CompilerParams(vmem_limit_bytes=24 << 20),
    )(
        place,
        *[
            pltpu.with_memory_space_constraint(array, pltpu.HBM)
            for array in (
                traces, jnp.asarray(forward_tables()), bin_slot.reshape(8, 128),
                pair_source, pair_receiver, pair_bin,
            )
        ],
    )


def pairs_kernel(block_ref, y_ref, out_ref, source_ref, placed_ref, row_ref):
    index = lax.broadcasted_iota(jnp.int32, (128, 128), 0).astype(F32).astype(BF)
    low_half = lax.broadcasted_iota(jnp.int32, (8, P_DEV), 0) < FG
    lower_row = (lax.broadcasted_iota(jnp.int32, (16, 128), 0) // 8).astype(F32)
    one, zero = jnp.ones((), BF), jnp.zeros((), BF)

    def spread(row):
        columns = []
        for q in range(row.shape[0]):
            entry = jnp.broadcast_to(row[q : q + 1], (16, 128)).astype(BF)
            entry = jnp.concatenate([entry] * 8, axis=0)
            columns.append(jnp.where(index == entry, one, zero))
        return jnp.concatenate(columns, axis=1)

    for s in range(STEPS):
        block = block_ref[s]
        for a in range(N_A):
            source_ref[a * ROWS : (a + 1) * ROWS, :] = y_ref[a, block, :ROWS, :]

        def body(c, carry):
            lists = [
                y_ref[kind, c, ROWS:, :].astype(F32)[s * QUARTERS : (s + 1) * QUARTERS]
                for kind in range(4)
            ]
            receiver = jnp.concatenate([y_ref[a, c, :ROWS, :] for a in range(N_A)], axis=0)
            pieces = []
            for q in range(0, QUARTERS, GROUPQ):
                width = GROUPQ * 128
                u = jnp.dot(
                    source_ref[...], spread(lists[0][q : q + GROUPQ]), preferred_element_type=F32
                )
                v = jnp.dot(
                    receiver, spread(lists[1][q : q + GROUPQ]), preferred_element_type=F32
                )
                real_part = jnp.zeros((8, width), F32)
                imag_part = jnp.zeros((8, width), F32)
                for a in range(N_A):
                    for r in range(0, HALF, 8):
                        at = a * ROWS + r
                        u_re, u_im = u[at : at + 8], u[at + HALF : at + HALF + 8]
                        v_re, v_im = v[at : at + 8], v[at + HALF : at + HALF + 8]
                        real_part += u_re * v_re + u_im * v_im
                        imag_part += u_re * v_im - u_im * v_re
                real_part += pltpu.roll(real_part, FG, axis=0)
                imag_part += pltpu.roll(imag_part, FG, axis=0)
                pieces.append(jnp.where(low_half[:, :width], real_part, imag_part))
            partial = jnp.concatenate(pieces, axis=1)
            partial = jnp.concatenate([partial, partial], axis=0).astype(BF)
            for q in range(QUARTERS):
                owner = (jnp.broadcast_to(lists[3][q : q + 1], (16, 128)) - lower_row).astype(BF)
                values = partial[:, q * 128 : (q + 1) * 128]
                lanes = pl.ds(pl.multiple_of(c * P_DEV + q * 128, 128), 128)
                for k in range(0, N_CHAN, 2):
                    placed_ref[k * 8 : k * 8 + 16, lanes] = jnp.where(
                        owner == jnp.full((16, 128), float(k), BF), values, zero
                    )
            row_ref[:, pl.ds(pl.multiple_of(c * P_DEV, 128), P_DEV)] = spread(lists[2])
            return carry

        lax.fori_loop(0, N_CHAN, body, 0, unroll=8)
        binned = lax.dot_general(
            placed_ref[...], row_ref[...], NT, preferred_element_type=F32
        ).astype(BF)
        for b in range(N_B):
            out_ref[b, :, s * BIN_DEV : (s + 1) * BIN_DEV] = binned


def bin_pairs(source_block, chunks):
    return pl.pallas_call(
        pairs_kernel,
        in_specs=[SMEM, VMEM],
        out_specs=VMEM,
        out_shape=jax.ShapeDtypeStruct((N_B, OWNED, STEPS * BIN_DEV), BF),
        scratch_shapes=[
            pltpu.VMEM((N_A * ROWS, CH_DEV), BF),
            pltpu.VMEM((OWNED, N_CHAN * P_DEV), BF),
            pltpu.VMEM((BIN_DEV, N_CHAN * P_DEV), BF),
        ],
        compiler_params=pltpu.CompilerParams(vmem_limit_bytes=32 << 20),
    )(source_block, chunks)


def sum_kernel(part_ref, out_ref):
    total = part_ref[0].astype(F32)
    for b in range(1, N_B):
        total += part_ref[b].astype(F32)
    total = total.astype(BF)
    for a in range(N_A):
        out_ref[a] = total


def sum_windows(parts):
    return pl.pallas_call(
        sum_kernel,
        in_specs=[VMEM],
        out_specs=VMEM,
        out_shape=jax.ShapeDtypeStruct((N_A, OWNED, STEPS * BIN_DEV), BF),
        compiler_params=pltpu.CompilerParams(vmem_limit_bytes=8 << 20),
    )(parts)


def lag_kernel(place_ref, bins_ref, cos_ref, sin_ref, first_ref, second_ref, out_hbm, out_ref, sem):
    place = place_ref[0]
    basis = (
        cos_ref[...] * first_ref[pl.ds(place, 1), :]
        + sin_ref[...] * second_ref[pl.ds(place, 1), :]
    )
    upper = basis.astype(BF)
    rest = (basis - upper.astype(F32)).astype(BF)
    copies = []
    for s in range(STEPS):
        bins = bins_ref[:, s * BIN_DEV : (s + 1) * BIN_DEV]
        out_ref[s] = jnp.dot(upper, bins, preferred_element_type=F32) + jnp.dot(
            rest, bins, preferred_element_type=F32
        )
        copies.append(pltpu.make_async_copy(out_ref.at[s], out_hbm.at[s], sem.at[s]))
        copies[s].start()
    for copy in copies:
        copy.wait()


def project_lags(place, bins):
    return pl.pallas_call(
        lag_kernel,
        in_specs=[SMEM] + [VMEM] * 5,
        out_specs=HBM,
        out_shape=jax.ShapeDtypeStruct((STEPS, LAGS // N_WIN, BIN_DEV), F32),
        scratch_shapes=[
            pltpu.VMEM((STEPS, LAGS // N_WIN, BIN_DEV), F32),
            pltpu.SemaphoreType.DMA((STEPS,)),
        ],
        compiler_params=pltpu.CompilerParams(vmem_limit_bytes=16 << 20),
    )(place, bins, *[jnp.asarray(t) for t in lag_tables()])


def on_device(traces, source_block, pair_source, pair_receiver, pair_bin, bin_slot):
    place = lax.axis_index(("b", "a")).reshape(1)
    chunks = whiten(place, traces, pair_source, pair_receiver, pair_bin, bin_slot)
    chunks = lax.all_to_all(chunks, ("a", "chan"), 0, 0, tiled=True)
    parts = bin_pairs(source_block, chunks.reshape(N_A, N_CHAN, ROWS + META, CH_DEV))
    parts = lax.all_to_all(parts, "b", 0, 0, tiled=True)
    bins = sum_windows(parts).reshape(GROUPS, COLS, STEPS * BIN_DEV)
    bins = lax.all_to_all(bins, ("a", "chan"), 0, 0, tiled=True)
    return project_lags(place, bins.reshape(2 * F, STEPS * BIN_DEV))


def solution(mesh):
    split = Mesh(mesh.devices.reshape(N_B, N_A, N_CHAN), ("b", "a", "chan"))
    win = ("b", "a")
    placed = (P(win, "chan", None), P(), P(None, "chan"), P(None, "chan"), P(None, "chan"), P())
    return jax.shard_map(
        on_device, mesh=split, in_specs=placed, out_specs=P(None, win, "chan"), check_vma=False
    )
```
